32 devices in a mesh: gx: 8 (over z, x), gy: 4 (over y, core).
Axes of the slice: x: 2, y: 2, z: 4, core: 2. Of those that a mesh axis runs over, the one named last changes fastest.
Arguments:
- increment: bfloat16 [64, 384, 512], P(None, 'gx', 'gy'), may hold values from -6 to 6
- ensemble: bfloat16 [4, 64, 384, 512], P(None, None, 'gx', 'gy'), may hold values from -6 to 6
- wind_u: bfloat16 [64, 384, 512], P(None, 'gx', 'gy'), may hold values from -0.94921875 to 0.94921875
- wind_v: bfloat16 [64, 384, 512], P(None, 'gx', 'gy'), may hold values from -0.94921875 to 0.94921875
- filter_length: float32 [64], replicated, may hold values from 8 to 3072
- jacobian: bfloat16 [32, 512, 64], P(('gx', 'gy')), may hold values from -0.75 to 0.75
- obs_weight: float32 [32, 512], P(('gx', 'gy')), may hold values from 0.1 to 1
- departure: bfloat16 [2048, 512, 128], P(('gx', 'gy')), may hold values from -6 to 6
- obs_home: int32 [2048], P(('gx', 'gy')), may hold values from 0 to 31, as said below
- obs_line: int32 [2048], P(('gx', 'gy')), may hold values from 0 to 47
- obs_count: int32 [2048], P(('gx', 'gy')), may hold values from 1 to 128
Outputs:
- grad_alpha: float32 [4, 64, 384, 512], P(None, None, 'gx', 'gy')
- grad_static: float32 [64, 384, 512], P(None, 'gx', 'gy')
The draws below stay inside these ranges and needn't reach their ends.
Inputs may be any that keep to these rules, and one draw needn't show every extreme that they name: `obs_home`: the records of one device name 32 distinct grid devices, each exactly 2 times.
All inputs are finite; a program needn't handle non-finite values.
Results may differ from the reference program's by a relative error of at most 0.003.
Values may be sent and summed in bfloat16 or wider, within the bound.
A program may use at most 192 MiB of HBM per device.

```python
import math
import jax
import jax.numpy as jnp
from jax import lax

CX = 48
CY = 128
LEV = 64
CH = 512
MEM = 4
OBS_DEV = 64
HOMES = 32
MOST = 2
NX = 384
NY = 512
RECORDS = 2048
N_GX = 8
N_GY = 4


def draw_obs_home(key, part):
    subkeys = jax.random.split(jax.random.fold_in(key, 17), 3)
    levels = jax.random.randint(subkeys[0], (HOMES,), 0, 4)
    weights = 1 + 3 * levels
    scores = jax.random.randint(subkeys[1], (HOMES, HOMES), 0, 4096) * weights[None, :]
    scores = scores * HOMES + jnp.arange(HOMES)[None, :]
    picked = lax.top_k(scores, OBS_DEV // MOST)[1]
    repeated = jnp.repeat(picked, MOST, axis=1)
    shuffle = jax.random.randint(subkeys[2], (HOMES, OBS_DEV), 0, 4096) * OBS_DEV + jnp.arange(OBS_DEV)[None, :]
    ordering = jnp.argsort(shuffle, axis=1, stable=True)
    return jnp.take_along_axis(repeated, ordering, axis=1).reshape(HOMES * OBS_DEV).astype(jnp.int32)


def touch_ends(array, stream_key, smallest, largest):
    extent = array.shape
    index_at = [jax.random.randint(jax.random.fold_in(stream_key, axis), (), 0, extent[axis]) for axis in range(len(extent))]
    array = array.at[tuple(index_at)].set(smallest)
    longest = extent.index(max(extent))
    index_at[longest] = (index_at[longest] + 1) % extent[longest]
    return array.at[tuple(index_at)].set(largest)


def shard_levels(key, shape, pieces, low, top_value):
    def one(position, shards_of):
        heights = jax.random.uniform(jax.random.fold_in(jax.random.fold_in(key, 6), position), (shards_of,), jnp.float32, low / len(pieces), top_value / len(pieces))
        return jnp.repeat(jnp.exp(heights), shape[position] // shards_of).reshape((-1,) + (1,) * (len(shape) - position - 1))

    level = one(*pieces[0])
    for cut in pieces[1:]:
        level = level * one(*cut)
    return level


def bell_draw(rng, shape, scale, bound, shards=(), held_as=jnp.bfloat16):
    drawn = scale * jax.random.normal(rng, shape, jnp.float32)
    if shards:
        drawn = drawn * shard_levels(rng, shape, shards, -0.22, 0.18)
    return jnp.clip(drawn, -bound, bound).astype(held_as)


def setup_inputs(seed: int = 0) -> dict:
    key_of = jax.random.split(jax.random.key(seed), 12)
    increment = bell_draw(key_of[0], (LEV, NX, NY), 1.0, 6.0, ((1, 8), (2, 4)))
    ensemble = bell_draw(key_of[1], (MEM, LEV, NX, NY), 1.0, 6.0, ((2, 8), (3, 4)))
    wind_u = jnp.clip(jax.random.uniform(key_of[2], (LEV, NX, NY), jnp.float32, -0.94921875, 0.94921875) * shard_levels(key_of[2], (LEV, NX, NY), ((1, 8), (2, 4)), -0.4, 0.0), -0.94921875, 0.94921875).astype(jnp.bfloat16)
    wind_v = jnp.clip(jax.random.uniform(key_of[3], (LEV, NX, NY), jnp.float32, -0.94921875, 0.94921875) * shard_levels(key_of[3], (LEV, NX, NY), ((1, 8), (2, 4)), -0.4, 0.0), -0.94921875, 0.94921875).astype(jnp.bfloat16)
    filter_length = jnp.clip(jnp.exp(jax.random.uniform(key_of[4], (LEV,), jnp.float32, math.log(8.0), math.log(3072.0))), 8.0, 3072.0)
    jacobian = bell_draw(key_of[5], (HOMES, CH, LEV), LEV ** -0.5, 0.75, ((0, 32),))
    obs_weight = jnp.clip(jnp.exp(math.log(1.0) - 2.3025851 * jax.random.uniform(key_of[6], (HOMES, CH), jnp.float32) ** shard_levels(key_of[6], (HOMES, CH), ((0, 32),), -0.2, 0.2)), 0.1, 1.0)
    departure = bell_draw(key_of[7], (RECORDS, CH, CY), 1.0, 6.0, ((0, 32),))
    obs_home = draw_obs_home(jax.random.fold_in(key_of[11], 71), 0)
    obs_line = touch_ends(jax.random.randint(key_of[9], (RECORDS,), 0, CX), jax.random.fold_in(key_of[9], 1), 0, CX - 1).astype(jnp.int32)
    obs_count = touch_ends(jax.random.randint(key_of[10], (RECORDS,), 1, CY + 1), jax.random.fold_in(key_of[10], 1), 1, CY).astype(jnp.int32)
    return dict(increment=increment, ensemble=ensemble, wind_u=wind_u, wind_v=wind_v, filter_length=filter_length, jacobian=jacobian, obs_weight=obs_weight, departure=departure, obs_home=obs_home, obs_line=obs_line, obs_count=obs_count)


def recursive(field, coefs, decays, backward):

    def advance(state, column):
        updated = coefs[:, None] * column + decays[:, None] * state
        return (updated, updated)
    start = jnp.zeros(field.shape[1:], jnp.float32)
    _, result = lax.scan(advance, start, field, reverse=backward)
    return result

def smooth(field, forward_coef, backward_coef, decays):
    turned = jnp.transpose(field, (1, 0, 2))
    turned = recursive(turned, forward_coef, decays, False)
    turned = recursive(turned, backward_coef, decays, True)
    turned = jnp.transpose(turned, (2, 1, 0))
    turned = recursive(turned, forward_coef, decays, False)
    turned = recursive(turned, backward_coef, decays, True)
    return jnp.transpose(turned, (1, 2, 0))

def transport_x(static, speed):
    padded = jnp.pad(static, ((0, 0), (1, 1), (0, 0)))
    return static + jnp.maximum(speed, 0.0) * (padded[:, :-2, :] - static) + jnp.maximum(-speed, 0.0) * (padded[:, 2:, :] - static)

def transport_y(static, speed):
    padded = jnp.pad(static, ((0, 0), (0, 0), (1, 1)))
    return static + jnp.maximum(speed, 0.0) * (padded[:, :, :-2] - static) + jnp.maximum(-speed, 0.0) * (padded[:, :, 2:] - static)

def one_home(packed):
    matrix, weight_row, gathered, observed_dep, counts = packed
    matrix = matrix.astype(jnp.float32)
    predicted = jnp.einsum('cl,oly->ocy', matrix, gathered.astype(jnp.float32))
    observed = (jnp.arange(CY, dtype=jnp.int32)[None, :] < counts[:, None]).astype(jnp.float32)
    weighted = (weight_row[None, :, None] * (predicted - observed_dep.astype(jnp.float32)) * observed[:, None, :]).astype(jnp.bfloat16)
    adjoint = jnp.einsum('cl,ocy->oly', matrix, weighted.astype(jnp.float32))
    return adjoint.astype(jnp.bfloat16)

def reference(increment, ensemble, wind_u, wind_v, filter_length, jacobian, obs_weight, departure, obs_home, obs_line, obs_count):
    home_count = N_GX * N_GY
    grid_x = obs_home // N_GY * CX + obs_line
    grid_y = obs_home % N_GY
    block_id = (grid_x * N_GY + grid_y).astype(jnp.int32)
    blocks = jnp.transpose(increment.reshape(LEV, NX, N_GY, CY), (1, 2, 0, 3)).reshape(NX * N_GY, LEV, CY)
    gathered = blocks[block_id].reshape(home_count, OBS_DEV, LEV, CY)
    adjoints = lax.map(one_home, (jacobian, obs_weight, gathered, departure.reshape(home_count, OBS_DEV, CH, CY), obs_count.reshape(home_count, OBS_DEV)))
    summed = jnp.zeros((NX * N_GY, LEV, CY), jnp.float32).at[block_id].add(adjoints.reshape(home_count * OBS_DEV, LEV, CY).astype(jnp.float32))
    grad_obs = jnp.transpose(summed.reshape(NX, N_GY, LEV, CY), (2, 0, 1, 3)).reshape(LEV, NX, NY)
    decays = jnp.exp(-1.0 / filter_length)
    forward_coef = jnp.sqrt(-jnp.expm1(-2.0 / filter_length))
    backward_coef = -jnp.expm1(-1.0 / filter_length)
    grad_alpha = lax.map(lambda member: smooth(member.astype(jnp.float32) * grad_obs, forward_coef, backward_coef, decays), ensemble)
    static = smooth(grad_obs, forward_coef, backward_coef, decays)
    speed_x = wind_u.astype(jnp.float32)
    speed_y = wind_v.astype(jnp.float32)
    for sweep_index in range(3):
        static = transport_x(static, speed_x)
        static = transport_y(static, speed_y)
    return (grad_alpha, static)
```

```python
import functools
import jax
import jax.numpy as jnp
from jax import lax
from jax.experimental import pallas as pl
from jax.experimental.pallas import tpu as pltpu
from jax.sharding import PartitionSpec as P

HALO = 3
EDGE = 8
highest = lax.Precision.HIGHEST


def peer_id(axes, index):
    if len(axes) == 1:
        return {axes[0]: index}
    minor = lax.axis_size(axes[1])
    return {axes[0]: index // minor, axes[1]: index % minor}


def gather_kernel(axes, scatter, x_ref, o_ref, send_sem, recv_sem, own_sem):
    count = lax.axis_size(axes)
    me = lax.axis_index(axes[0])
    for name in axes[1:]:
        me = me * lax.axis_size(name) + lax.axis_index(name)
    barrier = pltpu.get_barrier_semaphore()

    def greet(k, _):
        pl.semaphore_signal(
            barrier,
            inc=1,
            device_id=peer_id(axes, lax.rem(me + k, count)),
            device_id_type=pl.DeviceIdType.MESH,
        )
        return 0

    lax.fori_loop(1, count, greet, 0)
    own = pltpu.make_async_copy(x_ref.at[me] if scatter else x_ref, o_ref.at[me], own_sem)
    own.start()
    pl.semaphore_wait(barrier, count - 1)

    def copy(k, slot):
        to = lax.rem(me + k, count)
        return pltpu.make_async_remote_copy(
            src_ref=x_ref.at[to] if scatter else x_ref,
            dst_ref=o_ref.at[slot],
            send_sem=send_sem.at[k],
            recv_sem=recv_sem.at[k],
            device_id=peer_id(axes, to),
            device_id_type=pl.DeviceIdType.MESH,
        )

    def send(k, _):
        copy(k, me).start()
        return 0

    def finish(k, _):
        landed = copy(k, lax.rem(me + count - k, count))
        landed.wait_send()
        landed.wait_recv()
        return 0

    lax.fori_loop(1, count, send, 0)
    own.wait()
    lax.fori_loop(1, count, finish, 0)


def exchange(x, axes, collective_id, scatter):
    count = lax.axis_size(axes)
    shape = x.shape if scatter else (count,) + x.shape
    return pl.pallas_call(
        functools.partial(gather_kernel, axes, scatter),
        out_shape=jax.ShapeDtypeStruct(shape, x.dtype),
        in_specs=[pl.BlockSpec(memory_space=pltpu.VMEM)],
        out_specs=pl.BlockSpec(memory_space=pltpu.VMEM),
        scratch_shapes=[
            pltpu.SemaphoreType.DMA((count,)),
            pltpu.SemaphoreType.DMA((count,)),
            pltpu.SemaphoreType.DMA,
        ],
        compiler_params=pltpu.CompilerParams(
            collective_id=collective_id, has_side_effects=True
        ),
        name="exchange_%d" % collective_id,
    )(x)


def split(value):
    high = value.astype(jnp.bfloat16)
    return high, (value - high.astype(jnp.float32)).astype(jnp.bfloat16)


def local_kernel(members, g_ref, e_ref, mx_ref, wy_ref, x_ref, sx_ref, sy_ref, rows_ref):
    levels, cx, cy = g_ref.shape
    for l in range(levels):
        base = g_ref[l]
        parts = [base] + [e_ref[m, l].astype(jnp.float32) * base for m in range(members)]
        high, low = split(jnp.concatenate(parts, axis=1))
        result = jnp.dot(
            mx_ref[l],
            jnp.concatenate([high, high, low], axis=0),
            preferred_element_type=jnp.float32,
        )
        stack = jnp.concatenate(
            [result[:cx, m * cy : (m + 1) * cy] for m in range(members + 1)], axis=0
        )
        x_ref[l] = stack
        for m in range(members + 1):
            rows_ref[m, l : l + 1, :] = result[cx : cx + 1, m * cy : (m + 1) * cy]
            rows_ref[members + 1 + m, l : l + 1, :] = result[0:1, m * cy : (m + 1) * cy]
        high, low = split(stack)
        sums = lax.dot_general(
            wy_ref[l],
            jnp.concatenate([high, low], axis=1),
            (((1,), (1,)), ((), ())),
            preferred_element_type=jnp.float32,
        )
        sy_ref[l] = sums[0:8] + sums[8:16]
    sx_ref[...] = rows_ref[...].astype(sx_ref.dtype)


def final_kernel(members, x_ref, ux_ref, ex_ref, my_ref, uy_ref, ey_ref, a_ref, s_ref):
    levels = x_ref.shape[0]
    _, _, cx, cy = a_ref.shape
    first = (((0,), (0,)), ((), ()))
    for l in range(levels):
        field = x_ref[l] + lax.dot_general(
            ux_ref[l], ex_ref[l], first, precision=highest, preferred_element_type=jnp.float32
        )
        high, low = split(field)
        m_high, m_low = split(my_ref[l])
        weights = jnp.concatenate(
            [
                jnp.concatenate([m_high, m_low], axis=1),
                jnp.concatenate([m_high, jnp.zeros_like(m_low)], axis=1),
            ],
            axis=0,
        )
        both = jnp.dot(
            jnp.concatenate([high, low], axis=1), weights, preferred_element_type=jnp.float32
        )
        field = (
            both[:, :cy]
            + both[:, cy:]
            + lax.dot_general(
                ey_ref[l], uy_ref[l], first, precision=highest, preferred_element_type=jnp.float32
            )
        )
        s_ref[l] = field[:cx]
        for m in range(members):
            a_ref[m, l] = field[(m + 1) * cx : (m + 2) * cx]


def transport_kernel(s_ref, u_ref, v_ref, o_ref):
    levels, cx, cy = o_ref.shape
    rows, lanes = s_ref.shape[1:]
    for l in range(levels):
        s = s_ref[l]
        u = u_ref[l].astype(jnp.float32)
        v = v_ref[l].astype(jnp.float32)
        u_up, u_down = jnp.maximum(u, 0.0), jnp.maximum(-u, 0.0)
        v_up, v_down = jnp.maximum(v, 0.0), jnp.maximum(-v, 0.0)
        for _ in range(HALO):
            s = (
                s
                + u_up * (pltpu.roll(s, 1, 0) - s)
                + u_down * (pltpu.roll(s, rows - 1, 0) - s)
            )
            s = (
                s
                + v_up * (pltpu.roll(s, 1, 1) - s)
                + v_down * (pltpu.roll(s, lanes - 1, 1) - s)
            )
        o_ref[l] = s[EDGE : EDGE + cx, :cy]


def extended(cells):
    levels, cx, cy = cells.shape

    def shifts(axis):
        count = lax.axis_size(axis)
        return (
            [(i, i + 1) for i in range(count - 1)],
            [(i + 1, i) for i in range(count - 1)],
        )

    after, before = shifts("gx")
    top = lax.ppermute(jnp.moveaxis(cells[:, cx - HALO :, :], 1, 0), "gx", after)
    bottom = lax.ppermute(jnp.moveaxis(cells[:, :HALO, :], 1, 0), "gx", before)
    blank = jnp.zeros((levels, EDGE - HALO, cy), cells.dtype)
    rows = jnp.concatenate(
        [blank, jnp.moveaxis(top, 0, 1), cells, jnp.moveaxis(bottom, 0, 1), blank], axis=1
    )
    after, before = shifts("gy")
    left = lax.ppermute(jnp.moveaxis(rows[:, :, cy - HALO :], 2, 0), "gy", after)
    right = lax.ppermute(jnp.moveaxis(rows[:, :, :HALO], 2, 0), "gy", before)
    blank = jnp.zeros((levels, cx + 2 * EDGE, cy - 2 * HALO), cells.dtype)
    return jnp.concatenate(
        [rows, jnp.moveaxis(right, 0, 2), blank, jnp.moveaxis(left, 0, 2)], axis=2
    )


def smoother(lengths, count):
    pos = jnp.arange(count, dtype=jnp.float32)
    far = jnp.abs(pos[:, None] - pos[None, :])
    left = count - jnp.maximum(pos[:, None], pos[None, :])
    lengths = lengths[:, None, None]
    scale = -jnp.expm1(-1.0 / lengths) / jnp.sqrt(-jnp.expm1(-2.0 / lengths))
    return scale * jnp.exp(-far[None] / lengths) * -jnp.expm1(-2.0 * left[None] / lengths)


def end_weights(lengths, count):
    pos = jnp.arange(count, dtype=jnp.float32)
    coef = jnp.sqrt(-jnp.expm1(-2.0 / lengths))
    return coef[:, None] * jnp.exp(-(count - 1.0 - pos)[None, :] / lengths[:, None])


def responses(lengths, count):
    pos = jnp.arange(count, dtype=jnp.float32)[None, :]
    lengths = lengths[:, None]
    coef = -jnp.expm1(-1.0 / lengths)
    ratio = jnp.expm1(-2.0 * (count - pos) / lengths) / jnp.expm1(-2.0 / lengths)
    ahead = coef * jnp.exp(-(pos + 1.0) / lengths) * ratio
    behind = jnp.exp(-(count - pos) / lengths)
    return ahead, behind


def combine_weights(lengths, count, axis):
    size, me = lax.axis_size(axis), lax.axis_index(axis)
    link = responses(lengths, count)[0][:, 0]
    k = jnp.arange(size)

    def power(steps, ok):
        return jnp.where(
            ok[..., None],
            jnp.exp(-jnp.maximum(steps, 0)[..., None] * (count / lengths)),
            0.0,
        )

    ahead = power(me - 1 - k, k < me)
    behind = power(k - me - 1, k > me)
    pair = power(k[:, None] - 1 - k[None, :], k[None, :] < k[:, None])
    cross = link[None, :] * jnp.sum(behind[:, None, :] * pair, axis=0)
    return ahead, behind, cross


def body(
    increment,
    ensemble,
    wind_u,
    wind_v,
    filter_length,
    jacobian,
    obs_weight,
    departure,
    obs_home,
    obs_line,
    obs_count,
):
    axes = ("gx", "gy")
    home_count = lax.axis_size(axes)
    records_here = obs_home.shape[0]
    most = (records_here + home_count - 1) // home_count
    lev, cx, cy = increment.shape
    members = ensemble.shape[0]
    fields = members + 1
    slot_count = home_count * most
    onehot_home = (obs_home[:, None] == jnp.arange(home_count, dtype=jnp.int32)[None, :]).astype(
        jnp.int32
    )
    ranking = jnp.cumsum(onehot_home, axis=0) - 1
    rank_of = jnp.sum(onehot_home * ranking, axis=1)
    slot_of = obs_home * most + rank_of
    placing = slot_of[:, None] == jnp.arange(slot_count, dtype=jnp.int32)[None, :]
    requests = jnp.sum(placing.astype(jnp.int32) * (obs_line[:, None] + 1), axis=0) - 1
    wind = extended(jnp.concatenate([wind_u, wind_v], axis=0))
    asked_lines = lax.all_to_all(
        requests.reshape(home_count, most), axes, split_axis=0, concat_axis=0, tiled=True
    ).reshape(slot_count)
    select = (asked_lines[:, None] == jnp.arange(cx, dtype=jnp.int32)[None, :]).astype(
        jnp.bfloat16
    )
    outgoing = jnp.einsum(
        "sx,lxy->sly", select, increment, preferred_element_type=jnp.float32
    ).astype(jnp.bfloat16)
    arrived = lax.all_to_all(
        outgoing.reshape(home_count, most, lev, cy), axes, split_axis=0, concat_axis=0, tiled=True
    ).reshape(slot_count, lev, cy)
    gathered = jnp.take(arrived, slot_of, axis=0)
    matrix = jacobian[0]
    predicted = jnp.einsum("cl,oly->ocy", matrix, gathered, preferred_element_type=jnp.float32)
    observed = (jnp.arange(cy, dtype=jnp.int32)[None, :] < obs_count[:, None]).astype(jnp.float32)
    weighted = (
        obs_weight[0][None, :, None]
        * (predicted - departure.astype(jnp.float32))
        * observed[:, None, :]
    ).astype(jnp.bfloat16)
    adjoint = jnp.einsum(
        "cl,ocy->oly", matrix, weighted, preferred_element_type=jnp.float32
    ).astype(jnp.bfloat16)
    returning = jnp.einsum(
        "os,oly->sly", placing.astype(jnp.bfloat16), adjoint, preferred_element_type=jnp.float32
    ).astype(jnp.bfloat16)
    received = lax.all_to_all(
        returning.reshape(home_count, most, lev, cy), axes, split_axis=0, concat_axis=0, tiled=True
    ).reshape(slot_count, lev, cy)
    grad_obs = jnp.einsum("sx,sly->lxy", select, received, preferred_element_type=jnp.float32)

    tile = 16
    steps = lev // tile
    smooth_x = smoother(filter_length, cx)
    rows_x = jnp.concatenate(
        [
            smooth_x,
            end_weights(filter_length, cx)[:, None, :],
            jnp.zeros((lev, EDGE - 1, cx), jnp.float32),
        ],
        axis=1,
    )
    high_x = lax.reduce_precision(rows_x, 8, 7)
    cat_x = jnp.concatenate([high_x, rows_x - high_x, high_x], axis=2).astype(jnp.bfloat16)
    smooth_y = smoother(filter_length, cy)
    sums_y = jnp.stack([end_weights(filter_length, cy), smooth_y[:, 0, :]], axis=1)
    high_y = lax.reduce_precision(sums_y, 8, 7)
    low_y = sums_y - high_y
    blank = jnp.zeros((lev, 6, 2 * cy), jnp.float32)
    cat_y = jnp.concatenate(
        [
            jnp.concatenate([high_y, high_y], axis=2),
            blank,
            jnp.concatenate([low_y, jnp.zeros_like(low_y)], axis=2),
            blank,
        ],
        axis=1,
    ).astype(jnp.bfloat16)

    def levels_first(*shape):
        return pl.BlockSpec((tile,) + shape, lambda i: (i, 0, 0))

    params = pltpu.CompilerParams(
        dimension_semantics=("arbitrary",), vmem_limit_bytes=56 * 1024 * 1024
    )
    local, state_x, state_y = pl.pallas_call(
        functools.partial(local_kernel, members),
        grid=(steps,),
        in_specs=[
            levels_first(cx, cy),
            pl.BlockSpec((members, tile, cx, cy), lambda i: (0, i, 0, 0)),
            levels_first(cx + EDGE, 3 * cx),
            levels_first(16, 2 * cy),
        ],
        out_specs=[
            levels_first(fields * cx, cy),
            pl.BlockSpec((2 * fields, tile, cy), lambda i: (0, i, 0)),
            levels_first(8, fields * cx),
        ],
        out_shape=[
            jax.ShapeDtypeStruct((lev, fields * cx, cy), jnp.float32),
            jax.ShapeDtypeStruct((2 * fields, lev, cy), jnp.bfloat16),
            jax.ShapeDtypeStruct((lev, 8, fields * cx), jnp.float32),
        ],
        scratch_shapes=[pltpu.VMEM((2 * fields, tile, cy), jnp.float32)],
        compiler_params=params,
        name="local",
    )(grad_obs, ensemble, cat_x, cat_y)

    all_x = exchange(state_x, ("gx",), 1, False).astype(jnp.float32)
    ahead, behind, cross = combine_weights(filter_length, cx, "gx")
    enter_x = jnp.sum(ahead[:, None, :, None] * all_x[:, :fields], axis=0)
    leave_x = jnp.sum(
        behind[:, None, :, None] * all_x[:, fields:] + cross[:, None, :, None] * all_x[:, :fields],
        axis=0,
    )
    edges_x = jnp.stack([enter_x, leave_x], axis=0)
    out_x = jnp.stack(responses(filter_length, cx), axis=0)
    extra = jnp.sum(
        edges_x[:, :, :, None, :] * jnp.moveaxis(sums_y, 1, 1)[None, None], axis=-1
    )
    state_y = jnp.moveaxis(state_y[:, :2], 1, 0).reshape(2, lev, fields, cx) + sum(
        jnp.moveaxis(extra[s], (0, 1, 2), (2, 1, 0))[..., None] * out_x[s][None, :, None, :]
        for s in range(2)
    )
    all_y = exchange(
        state_y.reshape(2, lev, fields * cx).astype(jnp.bfloat16), ("gy",), 2, False
    ).astype(jnp.float32)
    ahead, behind, cross = combine_weights(filter_length, cy, "gy")
    enter_y = jnp.sum(ahead[:, :, None] * all_y[:, 0], axis=0)
    leave_y = jnp.sum(
        behind[:, :, None] * all_y[:, 1] + cross[:, :, None] * all_y[:, 0], axis=0
    )
    edges_y = jnp.concatenate(
        [jnp.stack([enter_y, leave_y], axis=1), jnp.zeros((lev, 6, fields * cx), jnp.float32)],
        axis=1,
    )
    out_y = jnp.concatenate(
        [jnp.stack(responses(filter_length, cy), axis=1), jnp.zeros((lev, 6, cy), jnp.float32)],
        axis=1,
    )
    depth = -(-2 * fields // 8) * 8
    same = jnp.eye(fields, dtype=jnp.float32)
    block_x = (
        jnp.moveaxis(out_x, 0, 1)[:, :, None, None, :] * same[None, None, :, :, None]
    ).reshape(lev, 2 * fields, fields * cx)
    block_x = jnp.pad(block_x, ((0, 0), (0, depth - 2 * fields), (0, 0)))
    edges_x = jnp.moveaxis(edges_x.reshape(2 * fields, lev, cy), 0, 1)
    edges_x = jnp.pad(edges_x, ((0, 0), (0, depth - 2 * fields), (0, 0)))
    grad_alpha, static = pl.pallas_call(
        functools.partial(final_kernel, members),
        grid=(steps,),
        in_specs=[
            levels_first(fields * cx, cy),
            levels_first(depth, fields * cx),
            levels_first(depth, cy),
            levels_first(cy, cy),
            levels_first(8, cy),
            levels_first(8, fields * cx),
        ],
        out_specs=[
            pl.BlockSpec((members, tile, cx, cy), lambda i: (0, i, 0, 0)),
            levels_first(cx, cy),
        ],
        out_shape=[
            jax.ShapeDtypeStruct((members, lev, cx, cy), jnp.float32),
            jax.ShapeDtypeStruct((lev, cx, cy), jnp.float32),
        ],
        compiler_params=params,
        name="final",
    )(local, block_x, edges_x, smooth_y, out_y, edges_y)

    wide = (cx + 2 * EDGE, 2 * cy)
    static = pl.pallas_call(
        transport_kernel,
        grid=(steps,),
        in_specs=[
            levels_first(*wide),
            levels_first(*wide),
            pl.BlockSpec((tile,) + wide, lambda i: (i + steps, 0, 0)),
        ],
        out_specs=levels_first(cx, cy),
        out_shape=jax.ShapeDtypeStruct((lev, cx, cy), jnp.float32),
        compiler_params=params,
        name="transport",
    )(extended(static), wind, wind)
    return (grad_alpha, static)


def solution(mesh):
    return jax.shard_map(
        body,
        mesh=mesh,
        in_specs=(
            P(None, "gx", "gy"),
            P(None, None, "gx", "gy"),
            P(None, "gx", "gy"),
            P(None, "gx", "gy"),
            P(),
            P(("gx", "gy"), None, None),
            P(("gx", "gy"), None),
            P(("gx", "gy"), None, None),
            P(("gx", "gy")),
            P(("gx", "gy")),
            P(("gx", "gy")),
        ),
        out_specs=(P(None, None, "gx", "gy"), P(None, "gx", "gy")),
        check_vma=False,
    )
```

```python
import functools
import jax
import jax.numpy as jnp
from jax import lax
from jax.experimental import pallas as pl
from jax.experimental.pallas import tpu as pltpu
from jax.sharding import PartitionSpec as P

HALO = 3
EDGE = 8
highest = lax.Precision.HIGHEST


def peer_id(axes, index):
    if len(axes) == 1:
        return {axes[0]: index}
    minor = lax.axis_size(axes[1])
    return {axes[0]: index // minor, axes[1]: index % minor}


def gather_kernel(axes, scatter, x_ref, o_ref, send_sem, recv_sem, own_sem):
    count = lax.axis_size(axes)
    me = lax.axis_index(axes[0])
    for name in axes[1:]:
        me = me * lax.axis_size(name) + lax.axis_index(name)
    barrier = pltpu.get_barrier_semaphore()

    def greet(k, _):
        pl.semaphore_signal(
            barrier,
            inc=1,
            device_id=peer_id(axes, lax.rem(me + k, count)),
            device_id_type=pl.DeviceIdType.MESH,
        )
        return 0

    lax.fori_loop(1, count, greet, 0)
    own = pltpu.make_async_copy(x_ref.at[me] if scatter else x_ref, o_ref.at[me], own_sem)
    own.start()
    pl.semaphore_wait(barrier, count - 1)

    def copy(k, slot):
        to = lax.rem(me + k, count)
        return pltpu.make_async_remote_copy(
            src_ref=x_ref.at[to] if scatter else x_ref,
            dst_ref=o_ref.at[slot],
            send_sem=send_sem.at[k],
            recv_sem=recv_sem.at[k],
            device_id=peer_id(axes, to),
            device_id_type=pl.DeviceIdType.MESH,
        )

    def send(k, _):
        copy(k, me).start()
        return 0

    def finish(k, _):
        landed = copy(k, lax.rem(me + count - k, count))
        landed.wait_send()
        landed.wait_recv()
        return 0

    lax.fori_loop(1, count, send, 0)
    own.wait()
    lax.fori_loop(1, count, finish, 0)


def exchange(x, axes, collective_id, scatter):
    count = lax.axis_size(axes)
    shape = x.shape if scatter else (count,) + x.shape
    return pl.pallas_call(
        functools.partial(gather_kernel, axes, scatter),
        out_shape=jax.ShapeDtypeStruct(shape, x.dtype),
        in_specs=[pl.BlockSpec(memory_space=pltpu.VMEM)],
        out_specs=pl.BlockSpec(memory_space=pltpu.VMEM),
        scratch_shapes=[
            pltpu.SemaphoreType.DMA((count,)),
            pltpu.SemaphoreType.DMA((count,)),
            pltpu.SemaphoreType.DMA,
        ],
        compiler_params=pltpu.CompilerParams(
            collective_id=collective_id, has_side_effects=True
        ),
        name="exchange_%d" % collective_id,
    )(x)


def split(value):
    high = value.astype(jnp.bfloat16)
    return high, (value - high.astype(jnp.float32)).astype(jnp.bfloat16)


def ways():
    return [(dx, dy) for dx in (-1, 0, 1) for dy in (-1, 0, 1) if (dx, dy) != (0, 0)]


def halo_kernel(low_x, high_x, low_y, high_y, from_x, from_y, send_sem, recv_sem):
    gx, gy = lax.axis_index("gx"), lax.axis_index("gy")
    size_x, size_y = lax.axis_size("gx"), lax.axis_size("gy")
    barrier = pltpu.get_barrier_semaphore()

    def present(dx, dy):
        x, y = gx + dx, gy + dy
        return (x >= 0) & (x < size_x) & (y >= 0) & (y < size_y)

    def copy(k, dx, dy):
        if dy == 0:
            source = high_x if dx == 1 else low_x
            target = from_x.at[0 if dx == 1 else 1]
        else:
            source = high_y if dy == 1 else low_y
            target = from_y.at[1 - dx, 0 if dy == 1 else 1]
        return pltpu.make_async_remote_copy(
            src_ref=source,
            dst_ref=target,
            send_sem=send_sem.at[k],
            recv_sem=recv_sem.at[k],
            device_id={"gx": gx + dx, "gy": gy + dy},
            device_id_type=pl.DeviceIdType.MESH,
        )

    around = 0
    for dx, dy in ways():
        around = around + present(dx, dy).astype(jnp.int32)

        @pl.when(present(dx, dy))
        def _():
            pl.semaphore_signal(
                barrier,
                inc=1,
                device_id={"gx": gx + dx, "gy": gy + dy},
                device_id_type=pl.DeviceIdType.MESH,
            )

    pl.semaphore_wait(barrier, around)
    for k, (dx, dy) in enumerate(ways()):

        @pl.when(present(dx, dy))
        def _():
            copy(k, dx, dy).start()

    for k, (dx, dy) in enumerate(ways()):

        @pl.when(jnp.logical_not(present(-dx, -dy)))
        def _():
            if dy == 0:
                slot = 0 if dx == 1 else 1
                from_x[slot] = jnp.zeros(from_x.shape[1:], from_x.dtype)
            else:
                slot = 0 if dy == 1 else 1
                from_y[1 - dx, slot] = jnp.zeros(from_y.shape[2:], from_y.dtype)

    for k, (dx, dy) in enumerate(ways()):

        @pl.when(present(dx, dy))
        def _():
            copy(k, dx, dy).wait_send()

        @pl.when(present(-dx, -dy))
        def _():
            copy(k, dx, dy).wait_recv()


def halo(low_x, high_x, low_y, high_y, collective_id):
    return pl.pallas_call(
        halo_kernel,
        out_shape=[
            jax.ShapeDtypeStruct((2,) + low_x.shape, low_x.dtype),
            jax.ShapeDtypeStruct((3, 2) + low_y.shape, low_y.dtype),
        ],
        in_specs=[pl.BlockSpec(memory_space=pltpu.VMEM)] * 4,
        out_specs=[pl.BlockSpec(memory_space=pltpu.VMEM)] * 2,
        scratch_shapes=[pltpu.SemaphoreType.DMA((8,)), pltpu.SemaphoreType.DMA((8,))],
        compiler_params=pltpu.CompilerParams(
            collective_id=collective_id, has_side_effects=True
        ),
        name="halo",
    )(low_x, high_x, low_y, high_y)


def edge_columns(cy):
    row = lax.broadcasted_iota(jnp.int32, (2 * EDGE, cy), 0)
    col = lax.broadcasted_iota(jnp.int32, (2 * EDGE, cy), 1)
    return (col == jnp.where(row < EDGE, row, row + cy - 2 * EDGE)).astype(jnp.bfloat16)


def local_kernel(members, g_ref, e_ref, mx_ref, wy_ref, x_ref, sx_ref, sy_ref, rows_ref):
    levels, cx, cy = g_ref.shape
    for l in range(levels):
        base = g_ref[l]
        parts = [base] + [e_ref[m, l].astype(jnp.float32) * base for m in range(members)]
        high, low = split(jnp.concatenate(parts, axis=1))
        result = jnp.dot(
            mx_ref[l],
            jnp.concatenate([high, high, low], axis=0),
            preferred_element_type=jnp.float32,
        )
        stack = jnp.concatenate(
            [result[:cx, m * cy : (m + 1) * cy] for m in range(members + 1)], axis=0
        )
        x_ref[l] = stack
        for m in range(members + 1):
            rows_ref[m, l : l + 1, :] = result[cx : cx + 1, m * cy : (m + 1) * cy]
            rows_ref[members + 1 + m, l : l + 1, :] = result[0:1, m * cy : (m + 1) * cy]
        high, low = split(stack)
        sums = lax.dot_general(
            wy_ref[l],
            jnp.concatenate([high, low], axis=1),
            (((1,), (1,)), ((), ())),
            preferred_element_type=jnp.float32,
        )
        sy_ref[l] = sums[0:8] + sums[8:16]
    sx_ref[...] = rows_ref[...].astype(sx_ref.dtype)


def final_kernel(
    members, x_ref, ux_ref, ex_ref, my_ref, uy_ref, ey_ref,
    a_ref, s_ref, low_x, high_x, low_y, high_y,
):
    levels = x_ref.shape[0]
    _, _, cx, cy = a_ref.shape
    first = (((0,), (0,)), ((), ()))
    columns = edge_columns(cy)
    for l in range(levels):
        field = x_ref[l] + lax.dot_general(
            ux_ref[l], ex_ref[l], first, preferred_element_type=jnp.float32
        )
        high, low = split(field)
        m_high, m_low = split(my_ref[l])
        weights = jnp.concatenate(
            [
                jnp.concatenate([m_high, m_low], axis=1),
                jnp.concatenate([m_high, jnp.zeros_like(m_low)], axis=1),
            ],
            axis=0,
        )
        both = jnp.dot(
            jnp.concatenate([high, low], axis=1), weights, preferred_element_type=jnp.float32
        )
        field = (
            both[:, :cy]
            + both[:, cy:]
            + lax.dot_general(ey_ref[l], uy_ref[l], first, preferred_element_type=jnp.float32)
        )
        static = field[:cx]
        s_ref[l] = static
        for m in range(members):
            a_ref[m, l] = field[(m + 1) * cx : (m + 2) * cx]
        low_x[l] = static[:EDGE].astype(low_x.dtype)
        high_x[l] = static[cx - EDGE :].astype(high_x.dtype)
        sides = lax.dot_general(
            columns,
            static.astype(jnp.bfloat16),
            (((1,), (1,)), ((), ())),
            preferred_element_type=jnp.float32,
        )
        low_y[l] = sides[:EDGE].astype(low_y.dtype)
        high_y[l] = sides[EDGE:].astype(high_y.dtype)


def transport_kernel(s_ref, hx_ref, hy_ref, u_ref, v_ref, o_ref):
    levels, cx, cy = o_ref.shape
    rows, lanes = u_ref.shape[1:]
    place = edge_columns(cy)
    for l in range(levels):
        strips = []
        for k in range(3):
            pair = jnp.concatenate(
                [hy_ref[k, 1, l].astype(jnp.float32), hy_ref[k, 0, l].astype(jnp.float32)], axis=0
            ).astype(jnp.bfloat16)
            strips.append(
                lax.dot_general(
                    pair, place, (((0,), (0,)), ((), ())), preferred_element_type=jnp.float32
                )
            )
        s = jnp.concatenate(
            [
                jnp.concatenate(
                    [
                        hx_ref[0, l].astype(jnp.float32),
                        s_ref[l],
                        hx_ref[1, l].astype(jnp.float32),
                    ],
                    axis=0,
                ),
                jnp.concatenate([strips[0][cx - EDGE :], strips[1], strips[2][:EDGE]], axis=0),
            ],
            axis=1,
        )
        u = u_ref[l].astype(jnp.float32)
        v = v_ref[l].astype(jnp.float32)
        east, north = u > 0.0, v > 0.0
        u, v = jnp.abs(u), jnp.abs(v)
        for _ in range(HALO):
            s = s + u * (jnp.where(east, pltpu.roll(s, 1, 0), pltpu.roll(s, rows - 1, 0)) - s)
            s = s + v * (jnp.where(north, pltpu.roll(s, 1, 1), pltpu.roll(s, lanes - 1, 1)) - s)
        o_ref[l] = s[EDGE : EDGE + cx, :cy]


def extended(cells):
    levels, cx, cy = cells.shape

    def shifts(axis):
        count = lax.axis_size(axis)
        return (
            [(i, i + 1) for i in range(count - 1)],
            [(i + 1, i) for i in range(count - 1)],
        )

    after, before = shifts("gx")
    top = lax.ppermute(jnp.moveaxis(cells[:, cx - HALO :, :], 1, 0), "gx", after)
    bottom = lax.ppermute(jnp.moveaxis(cells[:, :HALO, :], 1, 0), "gx", before)
    blank = jnp.zeros((levels, EDGE - HALO, cy), cells.dtype)
    rows = jnp.concatenate(
        [blank, jnp.moveaxis(top, 0, 1), cells, jnp.moveaxis(bottom, 0, 1), blank], axis=1
    )
    after, before = shifts("gy")
    left = lax.ppermute(jnp.moveaxis(rows[:, :, cy - HALO :], 2, 0), "gy", after)
    right = lax.ppermute(jnp.moveaxis(rows[:, :, :HALO], 2, 0), "gy", before)
    blank = jnp.zeros((levels, cx + 2 * EDGE, cy - 2 * HALO), cells.dtype)
    return jnp.concatenate(
        [rows, jnp.moveaxis(right, 0, 2), blank, jnp.moveaxis(left, 0, 2)], axis=2
    )


def smoother(lengths, count):
    pos = jnp.arange(count, dtype=jnp.float32)
    far = jnp.abs(pos[:, None] - pos[None, :])
    left = count - jnp.maximum(pos[:, None], pos[None, :])
    lengths = lengths[:, None, None]
    scale = -jnp.expm1(-1.0 / lengths) / jnp.sqrt(-jnp.expm1(-2.0 / lengths))
    return scale * jnp.exp(-far[None] / lengths) * -jnp.expm1(-2.0 * left[None] / lengths)


def end_weights(lengths, count):
    pos = jnp.arange(count, dtype=jnp.float32)
    coef = jnp.sqrt(-jnp.expm1(-2.0 / lengths))
    return coef[:, None] * jnp.exp(-(count - 1.0 - pos)[None, :] / lengths[:, None])


def responses(lengths, count):
    pos = jnp.arange(count, dtype=jnp.float32)[None, :]
    lengths = lengths[:, None]
    coef = -jnp.expm1(-1.0 / lengths)
    ratio = jnp.expm1(-2.0 * (count - pos) / lengths) / jnp.expm1(-2.0 / lengths)
    ahead = coef * jnp.exp(-(pos + 1.0) / lengths) * ratio
    behind = jnp.exp(-(count - pos) / lengths)
    return ahead, behind


def combine_weights(lengths, count, size, me):
    link = responses(lengths, count)[0][:, 0]
    k = jnp.arange(size)

    def power(steps, ok):
        return jnp.where(
            ok[..., None],
            jnp.exp(-jnp.maximum(steps, 0)[..., None] * (count / lengths)),
            0.0,
        )

    ahead = power(me - 1 - k, k < me)
    behind = power(k - me - 1, k > me)
    pair = power(k[:, None] - 1 - k[None, :], k[None, :] < k[:, None])
    cross = link[None, :] * jnp.sum(behind[:, None, :] * pair, axis=0)
    return ahead, behind, cross


def two_parts(value):
    high = lax.reduce_precision(value, 8, 7)
    return high, value - high


def whole_tiles(parts):
    joined = jnp.concatenate(parts, axis=1)
    return jnp.pad(joined, ((0, 0), (0, -joined.shape[1] % 16), (0, 0))).astype(jnp.bfloat16)


def left_terms(value):
    high, low = two_parts(value)
    return whole_tiles([high, low, high])


def right_terms(value):
    high, low = two_parts(value)
    return whole_tiles([high, high, low])


def body(
    increment,
    ensemble,
    wind_u,
    wind_v,
    filter_length,
    jacobian,
    obs_weight,
    departure,
    obs_home,
    obs_line,
    obs_count,
):
    axes = ("gx", "gy")
    home_count = lax.axis_size(axes)
    records_here = obs_home.shape[0]
    most = (records_here + home_count - 1) // home_count
    lev, cx, cy = increment.shape
    members = ensemble.shape[0]
    fields = members + 1
    slot_count = home_count * most
    onehot_home = (obs_home[:, None] == jnp.arange(home_count, dtype=jnp.int32)[None, :]).astype(
        jnp.int32
    )
    ranking = jnp.cumsum(onehot_home, axis=0) - 1
    rank_of = jnp.sum(onehot_home * ranking, axis=1)
    slot_of = obs_home * most + rank_of
    placing = slot_of[:, None] == jnp.arange(slot_count, dtype=jnp.int32)[None, :]
    requests = jnp.sum(placing.astype(jnp.int32) * (obs_line[:, None] + 1), axis=0) - 1
    wind = extended(jnp.concatenate([wind_u, wind_v], axis=0))
    asked_lines = exchange(
        jnp.pad(requests.reshape(home_count, 1, most), ((0, 0), (0, 7), (0, 128 - most))),
        axes,
        3,
        True,
    )[:, 0, :most].reshape(slot_count)
    select = (asked_lines[:, None] == jnp.arange(cx, dtype=jnp.int32)[None, :]).astype(
        jnp.bfloat16
    )
    outgoing = jnp.einsum(
        "sx,lxy->sly", select, increment, preferred_element_type=jnp.float32
    ).astype(jnp.bfloat16)
    arrived = lax.all_to_all(
        outgoing.reshape(home_count, most, lev, cy), axes, split_axis=0, concat_axis=0, tiled=True
    ).reshape(slot_count, lev, cy)
    arrived, wind = lax.optimization_barrier((arrived, wind))
    gathered = jnp.take(arrived, slot_of, axis=0)
    matrix = jacobian[0]
    predicted = jnp.einsum("cl,oly->ocy", matrix, gathered, preferred_element_type=jnp.float32)
    observed = (jnp.arange(cy, dtype=jnp.int32)[None, :] < obs_count[:, None]).astype(jnp.float32)
    weighted = (
        obs_weight[0][None, :, None]
        * (predicted - departure.astype(jnp.float32))
        * observed[:, None, :]
    ).astype(jnp.bfloat16)
    adjoint = jnp.einsum(
        "cl,ocy->oly", matrix, weighted, preferred_element_type=jnp.float32
    ).astype(jnp.bfloat16)
    returning = jnp.einsum(
        "os,oly->sly", placing.astype(jnp.bfloat16), adjoint, preferred_element_type=jnp.float32
    ).astype(jnp.bfloat16)
    received = lax.all_to_all(
        returning.reshape(home_count, most, lev, cy), axes, split_axis=0, concat_axis=0, tiled=True
    ).reshape(slot_count, lev, cy)
    grad_obs = jnp.einsum("sx,sly->lxy", select, received, preferred_element_type=jnp.float32)

    tile = 16
    steps = lev // tile
    smooth_x = smoother(filter_length, cx)
    rows_x = jnp.concatenate(
        [
            smooth_x,
            end_weights(filter_length, cx)[:, None, :],
            jnp.zeros((lev, EDGE - 1, cx), jnp.float32),
        ],
        axis=1,
    )
    high_x = lax.reduce_precision(rows_x, 8, 7)
    cat_x = jnp.concatenate([high_x, rows_x - high_x, high_x], axis=2).astype(jnp.bfloat16)
    smooth_y = smoother(filter_length, cy)
    sums_y = jnp.stack([end_weights(filter_length, cy), smooth_y[:, 0, :]], axis=1)
    high_y = lax.reduce_precision(sums_y, 8, 7)
    low_y = sums_y - high_y
    blank = jnp.zeros((lev, 6, 2 * cy), jnp.float32)
    cat_y = jnp.concatenate(
        [
            jnp.concatenate([high_y, high_y], axis=2),
            blank,
            jnp.concatenate([low_y, jnp.zeros_like(low_y)], axis=2),
            blank,
        ],
        axis=1,
    ).astype(jnp.bfloat16)

    def levels_first(*shape):
        return pl.BlockSpec((tile,) + shape, lambda i: (i, 0, 0))

    params = pltpu.CompilerParams(
        dimension_semantics=("arbitrary",), vmem_limit_bytes=56 * 1024 * 1024
    )
    local, state_x, state_y = pl.pallas_call(
        functools.partial(local_kernel, members),
        grid=(steps,),
        in_specs=[
            levels_first(cx, cy),
            pl.BlockSpec((members, tile, cx, cy), lambda i: (0, i, 0, 0)),
            levels_first(cx + EDGE, 3 * cx),
            levels_first(16, 2 * cy),
        ],
        out_specs=[
            levels_first(fields * cx, cy),
            pl.BlockSpec((2 * fields, tile, cy), lambda i: (0, i, 0)),
            levels_first(8, fields * cx),
        ],
        out_shape=[
            jax.ShapeDtypeStruct((lev, fields * cx, cy), jnp.float32),
            jax.ShapeDtypeStruct((2 * fields, lev, cy), jnp.bfloat16),
            jax.ShapeDtypeStruct((lev, 8, fields * cx), jnp.float32),
        ],
        scratch_shapes=[pltpu.VMEM((2 * fields, tile, cy), jnp.float32)],
        compiler_params=params,
        name="local",
    )(grad_obs, ensemble, cat_x, cat_y)

    size_x = lax.axis_size("gx")
    part = lev // size_x
    own = lax.axis_index("gx") * part
    mine = lax.dynamic_slice_in_dim(filter_length, own, part, 0)
    sent = jnp.moveaxis(state_x.reshape(2 * fields, size_x, part, cy), 1, 0)
    all_x = exchange(sent, ("gx",), 1, True).astype(jnp.float32)
    ahead, behind, cross = [
        jnp.stack(w) for w in zip(*[combine_weights(mine, cx, size_x, d) for d in range(size_x)])
    ]
    front, back = all_x[:, :fields], all_x[:, fields:]
    enter_x = sum(ahead[:, k, None, :, None] * front[k][None] for k in range(size_x))
    leave_x = sum(
        behind[:, k, None, :, None] * back[k][None] + cross[:, k, None, :, None] * front[k][None]
        for k in range(size_x)
    )
    swept = jnp.concatenate([enter_x, leave_x], axis=1).astype(jnp.bfloat16)
    swept = exchange(swept, ("gx",), 4, True).astype(jnp.float32)
    swept = jnp.moveaxis(swept, 0, 1).reshape(2, fields, lev, cy)
    enter_x, leave_x = swept[0], swept[1]
    edges_x = jnp.stack([enter_x, leave_x], axis=0)
    out_x = jnp.stack(responses(filter_length, cx), axis=0)
    extra = jnp.sum(
        edges_x[:, :, :, None, :] * jnp.moveaxis(sums_y, 1, 1)[None, None], axis=-1
    )
    state_y = jnp.moveaxis(state_y[:, :2], 1, 0).reshape(2, lev, fields, cx) + sum(
        jnp.moveaxis(extra[s], (0, 1, 2), (2, 1, 0))[..., None] * out_x[s][None, :, None, :]
        for s in range(2)
    )
    all_y = exchange(
        state_y.reshape(2, lev, fields * cx).astype(jnp.bfloat16), ("gy",), 2, False
    ).astype(jnp.float32)
    ahead, behind, cross = combine_weights(
        filter_length, cy, lax.axis_size("gy"), lax.axis_index("gy")
    )
    enter_y = jnp.sum(ahead[:, :, None] * all_y[:, 0], axis=0)
    leave_y = jnp.sum(
        behind[:, :, None] * all_y[:, 1] + cross[:, :, None] * all_y[:, 0], axis=0
    )
    edges_y = left_terms(jnp.stack([enter_y, leave_y], axis=1))
    out_y = right_terms(jnp.stack(responses(filter_length, cy), axis=1))
    same = jnp.eye(fields, dtype=jnp.float32)
    block_x = (
        jnp.moveaxis(out_x, 0, 1)[:, :, None, None, :] * same[None, None, :, :, None]
    ).reshape(lev, 2 * fields, fields * cx)
    block_x = left_terms(block_x)
    edges_x = right_terms(jnp.moveaxis(edges_x.reshape(2 * fields, lev, cy), 0, 1))
    depth_x, depth_y = block_x.shape[1], edges_y.shape[1]
    grad_alpha, static, *strips = pl.pallas_call(
        functools.partial(final_kernel, members),
        grid=(steps,),
        in_specs=[
            levels_first(fields * cx, cy),
            levels_first(depth_x, fields * cx),
            levels_first(depth_x, cy),
            levels_first(cy, cy),
            levels_first(depth_y, cy),
            levels_first(depth_y, fields * cx),
        ],
        out_specs=[
            pl.BlockSpec((members, tile, cx, cy), lambda i: (0, i, 0, 0)),
            levels_first(cx, cy),
            levels_first(EDGE, cy),
            levels_first(EDGE, cy),
            levels_first(EDGE, cx),
            levels_first(EDGE, cx),
        ],
        out_shape=[
            jax.ShapeDtypeStruct((members, lev, cx, cy), jnp.float32),
            jax.ShapeDtypeStruct((lev, cx, cy), jnp.float32),
            jax.ShapeDtypeStruct((lev, EDGE, cy), jnp.bfloat16),
            jax.ShapeDtypeStruct((lev, EDGE, cy), jnp.bfloat16),
            jax.ShapeDtypeStruct((lev, EDGE, cx), jnp.bfloat16),
            jax.ShapeDtypeStruct((lev, EDGE, cx), jnp.bfloat16),
        ],
        compiler_params=params,
        name="final",
    )(local, block_x, edges_x, smooth_y, out_y, edges_y)

    halo_x, halo_y = halo(*strips, 5)
    wide = (cx + 2 * EDGE, 2 * cy)
    static = pl.pallas_call(
        transport_kernel,
        grid=(steps,),
        in_specs=[
            levels_first(cx, cy),
            pl.BlockSpec((2, tile, EDGE, cy), lambda i: (0, i, 0, 0)),
            pl.BlockSpec((3, 2, tile, EDGE, cx), lambda i: (0, 0, i, 0, 0)),
            levels_first(*wide),
            pl.BlockSpec((tile,) + wide, lambda i: (i + steps, 0, 0)),
        ],
        out_specs=levels_first(cx, cy),
        out_shape=jax.ShapeDtypeStruct((lev, cx, cy), jnp.float32),
        compiler_params=params,
        name="transport",
    )(static, halo_x, halo_y, wind, wind)
    return (grad_alpha, static)


def solution(mesh):
    return jax.shard_map(
        body,
        mesh=mesh,
        in_specs=(
            P(None, "gx", "gy"),
            P(None, None, "gx", "gy"),
            P(None, "gx", "gy"),
            P(None, "gx", "gy"),
            P(),
            P(("gx", "gy"), None, None),
            P(("gx", "gy"), None),
            P(("gx", "gy"), None, None),
            P(("gx", "gy")),
            P(("gx", "gy")),
            P(("gx", "gy")),
        ),
        out_specs=(P(None, None, "gx", "gy"), P(None, "gx", "gy")),
        check_vma=False,
    )
```

```python
import functools
import jax
import jax.numpy as jnp
from jax import lax
from jax.experimental import pallas as pl
from jax.experimental.pallas import tpu as pltpu
from jax.sharding import PartitionSpec as P

HALO = 3
STRIP = 4
EDGE = 8
highest = lax.Precision.HIGHEST


def peer_id(axes, index):
    if len(axes) == 1:
        return {axes[0]: index}
    minor = lax.axis_size(axes[1])
    return {axes[0]: index // minor, axes[1]: index % minor}


def gather_kernel(axes, scatter, x_ref, o_ref, send_sem, recv_sem, own_sem):
    count = lax.axis_size(axes)
    me = lax.axis_index(axes[0])
    for name in axes[1:]:
        me = me * lax.axis_size(name) + lax.axis_index(name)
    barrier = pltpu.get_barrier_semaphore()

    def greet(k, _):
        pl.semaphore_signal(
            barrier,
            inc=1,
            device_id=peer_id(axes, lax.rem(me + k, count)),
            device_id_type=pl.DeviceIdType.MESH,
        )
        return 0

    lax.fori_loop(1, count, greet, 0)
    own = pltpu.make_async_copy(x_ref.at[me] if scatter else x_ref, o_ref.at[me], own_sem)
    own.start()
    pl.semaphore_wait(barrier, count - 1)

    def copy(k, slot):
        to = lax.rem(me + k, count)
        return pltpu.make_async_remote_copy(
            src_ref=x_ref.at[to] if scatter else x_ref,
            dst_ref=o_ref.at[slot],
            send_sem=send_sem.at[k],
            recv_sem=recv_sem.at[k],
            device_id=peer_id(axes, to),
            device_id_type=pl.DeviceIdType.MESH,
        )

    def send(k, _):
        copy(k, me).start()
        return 0

    def finish(k, _):
        landed = copy(k, lax.rem(me + count - k, count))
        landed.wait_send()
        landed.wait_recv()
        return 0

    lax.fori_loop(1, count, send, 0)
    own.wait()
    lax.fori_loop(1, count, finish, 0)


def exchange(x, axes, collective_id, scatter):
    count = lax.axis_size(axes)
    shape = x.shape if scatter else (count,) + x.shape
    return pl.pallas_call(
        functools.partial(gather_kernel, axes, scatter),
        out_shape=jax.ShapeDtypeStruct(shape, x.dtype),
        in_specs=[pl.BlockSpec(memory_space=pltpu.VMEM)],
        out_specs=pl.BlockSpec(memory_space=pltpu.VMEM),
        scratch_shapes=[
            pltpu.SemaphoreType.DMA((count,)),
            pltpu.SemaphoreType.DMA((count,)),
            pltpu.SemaphoreType.DMA,
        ],
        compiler_params=pltpu.CompilerParams(
            collective_id=collective_id, has_side_effects=True
        ),
        name="exchange_%d" % collective_id,
    )(x)


def split(value):
    high = value.astype(jnp.bfloat16)
    return high, (value - high.astype(jnp.float32)).astype(jnp.bfloat16)


def ways():
    return [(dx, dy) for dx in (-1, 0, 1) for dy in (-1, 0, 1) if (dx, dy) != (0, 0)]


def halo_kernel(low_x, high_x, low_y, high_y, from_x, from_y, send_sem, recv_sem):
    gx, gy = lax.axis_index("gx"), lax.axis_index("gy")
    size_x, size_y = lax.axis_size("gx"), lax.axis_size("gy")
    barrier = pltpu.get_barrier_semaphore()

    def present(dx, dy):
        x, y = gx + dx, gy + dy
        return (x >= 0) & (x < size_x) & (y >= 0) & (y < size_y)

    def copy(k, dx, dy):
        if dy == 0:
            source = high_x if dx == 1 else low_x
            target = from_x.at[0 if dx == 1 else 1]
        else:
            source = high_y if dy == 1 else low_y
            target = from_y.at[1 - dx, 0 if dy == 1 else 1]
        return pltpu.make_async_remote_copy(
            src_ref=source,
            dst_ref=target,
            send_sem=send_sem.at[k],
            recv_sem=recv_sem.at[k],
            device_id={"gx": gx + dx, "gy": gy + dy},
            device_id_type=pl.DeviceIdType.MESH,
        )

    around = 0
    for dx, dy in ways():
        around = around + present(dx, dy).astype(jnp.int32)

        @pl.when(present(dx, dy))
        def _():
            pl.semaphore_signal(
                barrier,
                inc=1,
                device_id={"gx": gx + dx, "gy": gy + dy},
                device_id_type=pl.DeviceIdType.MESH,
            )

    pl.semaphore_wait(barrier, around)
    for k, (dx, dy) in enumerate(ways()):

        @pl.when(present(dx, dy))
        def _():
            copy(k, dx, dy).start()

    for k, (dx, dy) in enumerate(ways()):

        @pl.when(jnp.logical_not(present(-dx, -dy)))
        def _():
            if dy == 0:
                slot = 0 if dx == 1 else 1
                from_x[slot] = jnp.zeros(from_x.shape[1:], from_x.dtype)
            else:
                slot = 0 if dy == 1 else 1
                from_y[1 - dx, slot] = jnp.zeros(from_y.shape[2:], from_y.dtype)

    for k, (dx, dy) in enumerate(ways()):

        @pl.when(present(dx, dy))
        def _():
            copy(k, dx, dy).wait_send()

        @pl.when(present(-dx, -dy))
        def _():
            copy(k, dx, dy).wait_recv()


def halo(low_x, high_x, low_y, high_y, collective_id):
    return pl.pallas_call(
        halo_kernel,
        out_shape=[
            jax.ShapeDtypeStruct((2,) + low_x.shape, low_x.dtype),
            jax.ShapeDtypeStruct((3, 2) + low_y.shape, low_y.dtype),
        ],
        in_specs=[pl.BlockSpec(memory_space=pltpu.VMEM)] * 4,
        out_specs=[pl.BlockSpec(memory_space=pltpu.VMEM)] * 2,
        scratch_shapes=[pltpu.SemaphoreType.DMA((8,)), pltpu.SemaphoreType.DMA((8,))],
        compiler_params=pltpu.CompilerParams(
            collective_id=collective_id, has_side_effects=True
        ),
        name="halo",
    )(low_x, high_x, low_y, high_y)


def edge_columns(cy, width):
    row = lax.broadcasted_iota(jnp.int32, (2 * width, cy), 0)
    col = lax.broadcasted_iota(jnp.int32, (2 * width, cy), 1)
    return (col == jnp.where(row < width, row, row + cy - 2 * width)).astype(jnp.bfloat16)


def local_kernel(members, g_ref, e_ref, mx_ref, wy_ref, x_ref, sx_ref, sy_ref, rows_ref):
    levels, cx, cy = g_ref.shape
    for l in range(levels):
        base = g_ref[l]
        parts = [base] + [e_ref[m, l].astype(jnp.float32) * base for m in range(members)]
        high, low = split(jnp.concatenate(parts, axis=1))
        result = jnp.dot(
            mx_ref[l],
            jnp.concatenate([high, high, low], axis=0),
            preferred_element_type=jnp.float32,
        )
        stack = jnp.concatenate(
            [result[:cx, m * cy : (m + 1) * cy] for m in range(members + 1)], axis=0
        )
        x_ref[l] = stack
        for m in range(members + 1):
            rows_ref[m, l : l + 1, :] = result[cx : cx + 1, m * cy : (m + 1) * cy]
            rows_ref[members + 1 + m, l : l + 1, :] = result[0:1, m * cy : (m + 1) * cy]
        high, low = split(stack)
        sums = lax.dot_general(
            wy_ref[l],
            jnp.concatenate([high, low], axis=1),
            (((1,), (1,)), ((), ())),
            preferred_element_type=jnp.float32,
        )
        sy_ref[l] = sums[0:8] + sums[8:16]
    sx_ref[...] = rows_ref[...].astype(sx_ref.dtype)


def final_kernel(
    members, x_ref, ux_ref, ex_ref, my_ref, uy_ref, ey_ref,
    a_ref, s_ref, low_x, high_x, low_y, high_y,
):
    levels = x_ref.shape[0]
    _, _, cx, cy = a_ref.shape
    first = (((0,), (0,)), ((), ()))
    columns = edge_columns(cy, STRIP)
    for l in range(levels):
        field = x_ref[l] + lax.dot_general(
            ux_ref[l], ex_ref[l], first, preferred_element_type=jnp.float32
        )
        high, low = split(field)
        m_high, m_low = split(my_ref[l])
        weights = jnp.concatenate(
            [
                jnp.concatenate([m_high, m_low], axis=1),
                jnp.concatenate([m_high, jnp.zeros_like(m_low)], axis=1),
            ],
            axis=0,
        )
        both = jnp.dot(
            jnp.concatenate([high, low], axis=1), weights, preferred_element_type=jnp.float32
        )
        field = (
            both[:, :cy]
            + both[:, cy:]
            + lax.dot_general(ey_ref[l], uy_ref[l], first, preferred_element_type=jnp.float32)
        )
        static = field[:cx]
        s_ref[l] = static
        for m in range(members):
            a_ref[m, l] = field[(m + 1) * cx : (m + 2) * cx]
        low_x[l] = static[:STRIP].astype(low_x.dtype)
        high_x[l] = static[cx - STRIP :].astype(high_x.dtype)
        sides = lax.dot_general(
            columns,
            static.astype(jnp.bfloat16),
            (((1,), (1,)), ((), ())),
            preferred_element_type=jnp.float32,
        )
        low_y[l] = sides[:STRIP].astype(low_y.dtype)
        high_y[l] = sides[STRIP:].astype(high_y.dtype)


def transport_kernel(
    s_ref, hx_ref, hy_ref, u_ref, v_ref, u_side, v_side, o_ref
):
    levels, cx, cy = o_ref.shape
    rows, lanes = u_ref.shape[1], 2 * cy
    blank = jnp.zeros((EDGE - STRIP, cy), jnp.float32)
    pad = [blank] if STRIP < EDGE else []
    place = edge_columns(cy, STRIP)
    for l in range(levels):
        strips = []
        for k in range(3):
            pair = jnp.concatenate(
                [hy_ref[k, 1, l].astype(jnp.float32), hy_ref[k, 0, l].astype(jnp.float32)], axis=0
            ).astype(jnp.bfloat16)
            strips.append(
                lax.dot_general(
                    pair, place, (((0,), (0,)), ((), ())), preferred_element_type=jnp.float32
                )
            )
        s = jnp.concatenate(
            [
                jnp.concatenate(
                    pad
                    + [
                        hx_ref[0, l].astype(jnp.float32),
                        s_ref[l],
                        hx_ref[1, l].astype(jnp.float32),
                    ]
                    + pad,
                    axis=0,
                ),
                jnp.concatenate([strips[0][cx - EDGE :], strips[1], strips[2][:EDGE]], axis=0),
            ],
            axis=1,
        )
        u = jnp.concatenate([u_ref[l], u_side[l]], axis=1).astype(jnp.float32)
        v = jnp.concatenate([v_ref[l], v_side[l]], axis=1).astype(jnp.float32)
        east, north = u > 0.0, v > 0.0
        u, v = jnp.abs(u), jnp.abs(v)
        for _ in range(HALO):
            s = s + u * (jnp.where(east, pltpu.roll(s, 1, 0), pltpu.roll(s, rows - 1, 0)) - s)
            s = s + v * (jnp.where(north, pltpu.roll(s, 1, 1), pltpu.roll(s, lanes - 1, 1)) - s)
        o_ref[l] = s[EDGE : EDGE + cx, :cy]


def extended(cells):
    levels, cx, cy = cells.shape

    def shifts(axis):
        count = lax.axis_size(axis)
        return (
            [(i, i + 1) for i in range(count - 1)],
            [(i + 1, i) for i in range(count - 1)],
        )

    after, before = shifts("gx")
    top = lax.ppermute(cells[:, cx - EDGE :, :], "gx", after)
    bottom = lax.ppermute(cells[:, :EDGE, :], "gx", before)
    rows = jnp.concatenate([top, cells, bottom], axis=1)
    columns = edge_columns(cy, EDGE)
    picked = jnp.einsum(
        "sy,lxy->lsx", columns, rows, preferred_element_type=jnp.float32
    ).astype(cells.dtype)
    after, before = shifts("gy")
    left = lax.ppermute(picked[:, EDGE:, :], "gy", after)
    right = lax.ppermute(picked[:, :EDGE, :], "gy", before)
    sides = jnp.einsum(
        "lsx,sy->lxy",
        jnp.concatenate([right, left], axis=1),
        columns,
        preferred_element_type=jnp.float32,
    ).astype(cells.dtype)
    return rows, sides


def smoother(lengths, count):
    pos = jnp.arange(count, dtype=jnp.float32)
    far = jnp.abs(pos[:, None] - pos[None, :])
    left = count - jnp.maximum(pos[:, None], pos[None, :])
    lengths = lengths[:, None, None]
    scale = -jnp.expm1(-1.0 / lengths) / jnp.sqrt(-jnp.expm1(-2.0 / lengths))
    return scale * jnp.exp(-far[None] / lengths) * -jnp.expm1(-2.0 * left[None] / lengths)


def end_weights(lengths, count):
    pos = jnp.arange(count, dtype=jnp.float32)
    coef = jnp.sqrt(-jnp.expm1(-2.0 / lengths))
    return coef[:, None] * jnp.exp(-(count - 1.0 - pos)[None, :] / lengths[:, None])


def responses(lengths, count):
    pos = jnp.arange(count, dtype=jnp.float32)[None, :]
    lengths = lengths[:, None]
    coef = -jnp.expm1(-1.0 / lengths)
    ratio = jnp.expm1(-2.0 * (count - pos) / lengths) / jnp.expm1(-2.0 / lengths)
    ahead = coef * jnp.exp(-(pos + 1.0) / lengths) * ratio
    behind = jnp.exp(-(count - pos) / lengths)
    return ahead, behind


def combine_weights(lengths, count, size, me):
    link = responses(lengths, count)[0][:, 0]
    k = jnp.arange(size)

    def power(steps, ok):
        return jnp.where(
            ok[..., None],
            jnp.exp(-jnp.maximum(steps, 0)[..., None] * (count / lengths)),
            0.0,
        )

    ahead = power(me - 1 - k, k < me)
    behind = power(k - me - 1, k > me)
    pair = power(k[:, None] - 1 - k[None, :], k[None, :] < k[:, None])
    cross = link[None, :] * jnp.sum(behind[:, None, :] * pair, axis=0)
    return ahead, behind, cross


def two_parts(value):
    high = lax.reduce_precision(value, 8, 7)
    return high, value - high


def whole_tiles(parts):
    joined = jnp.concatenate(parts, axis=1)
    return jnp.pad(joined, ((0, 0), (0, -joined.shape[1] % 16), (0, 0))).astype(jnp.bfloat16)


def left_terms(value):
    high, low = two_parts(value)
    return whole_tiles([high, low, high])


def right_terms(value):
    high, low = two_parts(value)
    return whole_tiles([high, high, low])


def body(
    increment,
    ensemble,
    wind_u,
    wind_v,
    filter_length,
    jacobian,
    obs_weight,
    departure,
    obs_home,
    obs_line,
    obs_count,
):
    axes = ("gx", "gy")
    home_count = lax.axis_size(axes)
    records_here = obs_home.shape[0]
    most = (records_here + home_count - 1) // home_count
    lev, cx, cy = increment.shape
    members = ensemble.shape[0]
    fields = members + 1
    slot_count = home_count * most
    onehot_home = (obs_home[:, None] == jnp.arange(home_count, dtype=jnp.int32)[None, :]).astype(
        jnp.int32
    )
    ranking = jnp.cumsum(onehot_home, axis=0) - 1
    rank_of = jnp.sum(onehot_home * ranking, axis=1)
    slot_of = obs_home * most + rank_of
    placing = slot_of[:, None] == jnp.arange(slot_count, dtype=jnp.int32)[None, :]
    requests = jnp.sum(placing.astype(jnp.int32) * (obs_line[:, None] + 1), axis=0) - 1
    asked_lines = exchange(
        jnp.pad(requests.reshape(home_count, 1, most), ((0, 0), (0, 7), (0, 128 - most))),
        axes,
        3,
        True,
    )[:, 0, :most].reshape(slot_count)
    select = (asked_lines[:, None] == jnp.arange(cx, dtype=jnp.int32)[None, :]).astype(
        jnp.bfloat16
    )
    outgoing = jnp.einsum(
        "sx,lxy->sly", select, increment, preferred_element_type=jnp.float32
    ).astype(jnp.bfloat16)
    arrived = lax.all_to_all(
        outgoing.reshape(home_count, most, lev, cy), axes, split_axis=0, concat_axis=0, tiled=True
    ).reshape(slot_count, lev, cy)
    smooth_x = smoother(filter_length, cx)
    rows_x = jnp.concatenate(
        [
            smooth_x,
            end_weights(filter_length, cx)[:, None, :],
            jnp.zeros((lev, EDGE - 1, cx), jnp.float32),
        ],
        axis=1,
    )
    high_x = lax.reduce_precision(rows_x, 8, 7)
    cat_x = jnp.concatenate([high_x, rows_x - high_x, high_x], axis=2).astype(jnp.bfloat16)
    smooth_y = smoother(filter_length, cy)
    sums_y = jnp.stack([end_weights(filter_length, cy), smooth_y[:, 0, :]], axis=1)
    high_y = lax.reduce_precision(sums_y, 8, 7)
    low_y = sums_y - high_y
    blank = jnp.zeros((lev, 6, 2 * cy), jnp.float32)
    cat_y = jnp.concatenate(
        [
            jnp.concatenate([high_y, high_y], axis=2),
            blank,
            jnp.concatenate([low_y, jnp.zeros_like(low_y)], axis=2),
            blank,
        ],
        axis=1,
    ).astype(jnp.bfloat16)

    out_x = jnp.stack(responses(filter_length, cx), axis=0)
    same = jnp.eye(fields, dtype=jnp.float32)
    block_x = left_terms(
        (
            jnp.moveaxis(out_x, 0, 1)[:, :, None, None, :] * same[None, None, :, :, None]
        ).reshape(lev, 2 * fields, fields * cx)
    )
    out_y = right_terms(jnp.stack(responses(filter_length, cy), axis=1))
    arrived, cat_x, cat_y, smooth_y, block_x, out_y = lax.optimization_barrier(
        (arrived, cat_x, cat_y, smooth_y, block_x, out_y)
    )
    gathered = jnp.take(arrived, slot_of, axis=0)
    matrix = jacobian[0]
    predicted = jnp.einsum("cl,oly->ocy", matrix, gathered, preferred_element_type=jnp.float32)
    observed = (jnp.arange(cy, dtype=jnp.int32)[None, :] < obs_count[:, None]).astype(jnp.float32)
    weighted = (
        obs_weight[0][None, :, None]
        * (predicted - departure.astype(jnp.float32))
        * observed[:, None, :]
    ).astype(jnp.bfloat16)
    adjoint = jnp.einsum(
        "cl,ocy->oly", matrix, weighted, preferred_element_type=jnp.float32
    ).astype(jnp.bfloat16)
    returning = jnp.einsum(
        "os,oly->sly", placing.astype(jnp.bfloat16), adjoint, preferred_element_type=jnp.float32
    ).astype(jnp.bfloat16)
    returning, winds = lax.optimization_barrier((returning, (wind_u, wind_v)))
    wind = extended(jnp.concatenate(winds, axis=0))
    received = lax.all_to_all(
        returning.reshape(home_count, most, lev, cy), axes, split_axis=0, concat_axis=0, tiled=True
    ).reshape(slot_count, lev, cy)
    received, (wind_rows, wind_sides) = lax.optimization_barrier((received, wind))
    grad_obs = jnp.einsum("sx,sly->lxy", select, received, preferred_element_type=jnp.float32)

    tile = 16
    steps = lev // tile
    def levels_first(*shape):
        return pl.BlockSpec((tile,) + shape, lambda i: (i, 0, 0))

    params = pltpu.CompilerParams(
        dimension_semantics=("arbitrary",), vmem_limit_bytes=56 * 1024 * 1024
    )
    local, state_x, state_y = pl.pallas_call(
        functools.partial(local_kernel, members),
        grid=(steps,),
        in_specs=[
            levels_first(cx, cy),
            pl.BlockSpec((members, tile, cx, cy), lambda i: (0, i, 0, 0)),
            levels_first(cx + EDGE, 3 * cx),
            levels_first(16, 2 * cy),
        ],
        out_specs=[
            levels_first(fields * cx, cy),
            pl.BlockSpec((2 * fields, tile, cy), lambda i: (0, i, 0)),
            levels_first(8, fields * cx),
        ],
        out_shape=[
            jax.ShapeDtypeStruct((lev, fields * cx, cy), jnp.float32),
            jax.ShapeDtypeStruct((2 * fields, lev, cy), jnp.bfloat16),
            jax.ShapeDtypeStruct((lev, 8, fields * cx), jnp.float32),
        ],
        scratch_shapes=[pltpu.VMEM((2 * fields, tile, cy), jnp.float32)],
        compiler_params=params,
        name="local",
    )(grad_obs, ensemble, cat_x, cat_y)

    size_x = lax.axis_size("gx")
    part = lev // size_x
    own = lax.axis_index("gx") * part
    mine = lax.dynamic_slice_in_dim(filter_length, own, part, 0)
    sent = jnp.moveaxis(state_x.reshape(2 * fields, size_x, part, cy), 1, 0)
    all_x = exchange(sent, ("gx",), 1, True).astype(jnp.float32)
    ahead, behind, cross = [
        jnp.stack(w) for w in zip(*[combine_weights(mine, cx, size_x, d) for d in range(size_x)])
    ]
    front, back = all_x[:, :fields], all_x[:, fields:]
    enter_x = sum(ahead[:, k, None, :, None] * front[k][None] for k in range(size_x))
    leave_x = sum(
        behind[:, k, None, :, None] * back[k][None] + cross[:, k, None, :, None] * front[k][None]
        for k in range(size_x)
    )
    swept = jnp.concatenate([enter_x, leave_x], axis=1).astype(jnp.bfloat16)
    swept = exchange(swept, ("gx",), 4, True).astype(jnp.float32)
    swept = jnp.moveaxis(swept, 0, 1).reshape(2, fields, lev, cy)
    enter_x, leave_x = swept[0], swept[1]
    edges_x = jnp.stack([enter_x, leave_x], axis=0)
    extra = jnp.sum(
        edges_x[:, :, :, None, :] * jnp.moveaxis(sums_y, 1, 1)[None, None], axis=-1
    )
    state_y = jnp.moveaxis(state_y[:, :2], 1, 0).reshape(2, lev, fields, cx) + sum(
        jnp.moveaxis(extra[s], (0, 1, 2), (2, 1, 0))[..., None] * out_x[s][None, :, None, :]
        for s in range(2)
    )
    all_y = exchange(
        state_y.reshape(2, lev, fields * cx).astype(jnp.bfloat16), ("gy",), 2, False
    ).astype(jnp.float32)
    ahead, behind, cross = combine_weights(
        filter_length, cy, lax.axis_size("gy"), lax.axis_index("gy")
    )
    enter_y = jnp.sum(ahead[:, :, None] * all_y[:, 0], axis=0)
    leave_y = jnp.sum(
        behind[:, :, None] * all_y[:, 1] + cross[:, :, None] * all_y[:, 0], axis=0
    )
    edges_y = left_terms(jnp.stack([enter_y, leave_y], axis=1))
    edges_x = right_terms(jnp.moveaxis(edges_x.reshape(2 * fields, lev, cy), 0, 1))
    depth_x, depth_y = block_x.shape[1], edges_y.shape[1]
    grad_alpha, static, *strips = pl.pallas_call(
        functools.partial(final_kernel, members),
        grid=(steps,),
        in_specs=[
            levels_first(fields * cx, cy),
            levels_first(depth_x, fields * cx),
            levels_first(depth_x, cy),
            levels_first(cy, cy),
            levels_first(depth_y, cy),
            levels_first(depth_y, fields * cx),
        ],
        out_specs=[
            pl.BlockSpec((members, tile, cx, cy), lambda i: (0, i, 0, 0)),
            levels_first(cx, cy),
            levels_first(STRIP, cy),
            levels_first(STRIP, cy),
            levels_first(STRIP, cx),
            levels_first(STRIP, cx),
        ],
        out_shape=[
            jax.ShapeDtypeStruct((members, lev, cx, cy), jnp.float32),
            jax.ShapeDtypeStruct((lev, cx, cy), jnp.float32),
            jax.ShapeDtypeStruct((lev, STRIP, cy), jnp.bfloat16),
            jax.ShapeDtypeStruct((lev, STRIP, cy), jnp.bfloat16),
            jax.ShapeDtypeStruct((lev, STRIP, cx), jnp.bfloat16),
            jax.ShapeDtypeStruct((lev, STRIP, cx), jnp.bfloat16),
        ],
        compiler_params=params,
        name="final",
    )(local, block_x, edges_x, smooth_y, out_y, edges_y)

    halo_x, halo_y = halo(*strips, 5)
    wide = (cx + 2 * EDGE, cy)
    static = pl.pallas_call(
        transport_kernel,
        grid=(steps,),
        in_specs=[
            levels_first(cx, cy),
            pl.BlockSpec((2, tile, STRIP, cy), lambda i: (0, i, 0, 0)),
            pl.BlockSpec((3, 2, tile, STRIP, cx), lambda i: (0, 0, i, 0, 0)),
            levels_first(*wide),
            pl.BlockSpec((tile,) + wide, lambda i: (i + steps, 0, 0)),
            levels_first(*wide),
            pl.BlockSpec((tile,) + wide, lambda i: (i + steps, 0, 0)),
        ],
        out_specs=levels_first(cx, cy),
        out_shape=jax.ShapeDtypeStruct((lev, cx, cy), jnp.float32),
        compiler_params=params,
        name="transport",
    )(static, halo_x, halo_y, wind_rows, wind_rows, wind_sides, wind_sides)
    return (grad_alpha, static)


def solution(mesh):
    return jax.shard_map(
        body,
        mesh=mesh,
        in_specs=(
            P(None, "gx", "gy"),
            P(None, None, "gx", "gy"),
            P(None, "gx", "gy"),
            P(None, "gx", "gy"),
            P(),
            P(("gx", "gy"), None, None),
            P(("gx", "gy"), None),
            P(("gx", "gy"), None, None),
            P(("gx", "gy")),
            P(("gx", "gy")),
            P(("gx", "gy")),
        ),
        out_specs=(P(None, None, "gx", "gy"), P(None, "gx", "gy")),
        check_vma=False,
    )
```
